32 devices in a mesh: groups: 2 (over y), ctx: 8 (over z, x), tp: 2 (over core).
Axes of the slice: x: 2, y: 2, z: 4, core: 2. Of those that a mesh axis runs over, the one named last changes fastest.
Arguments:
- normed_input: bfloat16 [4096, 2688], P(('groups', 'ctx')), parts along dimension 0, may hold values from -6 to 6
- attn_queries: bfloat16 [4096, 2048], P(('groups', 'ctx'), 'tp'), parts along dimension 0, may hold values from -45 to 45
- attn_keys: bfloat16 [4096, 1024], P(('groups', 'ctx'), 'tp'), parts along dimension 0, may hold values from -9 to 9
- attn_values: bfloat16 [4096, 1024], P(('groups', 'ctx'), 'tp'), parts along dimension 0, may hold values from -6 to 6
- out_grad: bfloat16 [4096, 2048], P(('groups', 'ctx'), 'tp'), parts along dimension 0, may hold values from -6 to 6
Outputs:
- query_grad: bfloat16 [4096, 2048], P(('groups', 'ctx'), 'tp'), parts along dimension 0
- key_weight_grad: float32 [5376, 1024], P(('groups', 'ctx'), 'tp'), parts along dimension 0
- value_grad: bfloat16 [4096, 1024], P(('groups', 'ctx'), 'tp'), parts along dimension 0
The draws below stay inside these ranges and needn't reach their ends.
There are 2 independent parts, one for each index of `groups`. The reference program is written for one: setup_inputs(seed, part) draws one part's arguments, and reference() takes and returns one part's arrays. A program takes and returns all parts, laid end to end along the dimension named above; each array names one. Nothing has to cross between parts.
All inputs are finite; a program needn't handle non-finite values.
Results may differ from the reference program's by a relative error of at most 0.0053.
Values may be sent and summed in bfloat16 or wider, within the bound.
No kernel may reach another device: no remote copies, remote signals or barrier semaphores. Data moves between devices by JAX's collectives and lax.ppermute only.
A program may use at most 128 MiB of HBM per device.

```python
import jax
import jax.numpy as jnp
from jax import lax

D = 2688
HD = 128
HQ = 16
HK = 8
W = 1024
TOKENS = 2048


def paired_draw(base_key):
    query_seed = jax.random.fold_in(base_key, 101)
    keys_seed = jax.random.fold_in(base_key, 202)
    key_part = jax.random.truncated_normal(keys_seed, -4.0, 4.0, (TOKENS, HK * HD), jnp.float32)
    query_part = jax.random.truncated_normal(query_seed, -4.0, 4.0, (TOKENS, HQ * HD), jnp.float32)
    return (query_part, key_part)


def draw_attn_queries(key, part):
    return paired_draw(key)[0].astype(jnp.bfloat16)


def draw_attn_keys(key, part):
    return paired_draw(key)[1].astype(jnp.bfloat16)


def with_spikes(array, key, source, target, blocks, factor):
    def block_of(axis_at):
        return (jnp.arange(array.shape[axis_at]) // (array.shape[axis_at] // blocks)).reshape((-1,) + (1,) * (array.ndim - 1 - axis_at))

    near = jax.random.permutation(key, blocks)[block_of(target)]
    other_side = (block_of(target) + blocks // 2) % blocks
    return jnp.where((block_of(source) == near) | (block_of(source) == other_side), factor * array, array)


def levels(stream_key, shape, split, least, high):
    loudness, own = 1.0, jax.random.fold_in(stream_key, 6)
    for position, blocks in split:
        draws = jnp.exp(jax.random.uniform(jax.random.fold_in(own, position), (blocks,), jnp.float32, least / len(split), high / len(split)))
        loudness = loudness * jnp.repeat(draws, shape[position] // blocks).reshape([-1 if axis == position else 1 for axis in range(len(shape))])
    return loudness


def noise(own_key, extent, deviation, reach, split=(), kind=jnp.bfloat16):
    values = deviation * jax.random.normal(own_key, extent, jnp.float32)
    if split:
        values = values * levels(own_key, extent, split, -0.22, 0.18)
    return jnp.clip(values, -reach, reach).astype(kind)


def noise_with(key, dims, width, limit, split, heavy, kind=jnp.bfloat16):
    array = width * jax.random.normal(key, dims, jnp.float32)
    if split:
        array = array * levels(key, dims, split, -0.22, 0.18)
    return jnp.clip(with_spikes(array, jax.random.fold_in(key, 3), *heavy), -limit, limit).astype(kind)


def setup_inputs(seed: int = 0, part: int = 0) -> dict:
    arg_keys = jax.random.split(jax.random.key(seed), 6)
    part_splits = jax.random.split(jax.random.fold_in(arg_keys[5], part), 6)
    return {
        "normed_input": noise_with(part_splits[0], (TOKENS, D), 1.0, 6.0, ((0, 8),), (0, 1, 8, 2.0)),
        "attn_queries": draw_attn_queries(jax.random.fold_in(jax.random.fold_in(arg_keys[5], part), 71), part),
        "attn_keys": draw_attn_keys(jax.random.fold_in(jax.random.fold_in(arg_keys[5], part), 71), part),
        "attn_values": noise(part_splits[3], (TOKENS, HK * HD), 1.0, 6.0, ((0, 8), (1, 2))),
        "out_grad": noise(part_splits[4], (TOKENS, HQ * HD), 1.0, 6.0, ((0, 8), (1, 2))),
    }


attn_scale = 168.0 ** -0.5


def reference(normed_input, attn_queries, attn_keys, attn_values, out_grad):
    group_size = HQ // HK
    block_rows = min(512, TOKENS)
    window_rows = block_rows + W
    kv_width = HK * HD
    pad_keys = jnp.concatenate([jnp.zeros((W, kv_width), jnp.bfloat16), attn_keys], axis=0)
    pad_values = jnp.concatenate([jnp.zeros((W, kv_width), jnp.bfloat16), attn_values], axis=0)
    query_offsets = jnp.arange(block_rows, dtype=jnp.int32)
    key_offsets = jnp.arange(window_rows, dtype=jnp.int32)

    def one_block(carry, block_index):
        key_total, value_total = carry
        row_start = (block_index * block_rows).astype(jnp.int32)
        query_block = lax.dynamic_slice_in_dim(attn_queries, row_start, block_rows, 0).astype(jnp.float32).reshape(block_rows, HK, group_size, HD)
        grad_block = lax.dynamic_slice_in_dim(out_grad, row_start, block_rows, 0).astype(jnp.float32).reshape(block_rows, HK, group_size, HD)
        key_block = lax.dynamic_slice_in_dim(pad_keys, row_start, window_rows, 0).astype(jnp.float32).reshape(window_rows, HK, HD)
        value_block = lax.dynamic_slice_in_dim(pad_values, row_start, window_rows, 0).astype(jnp.float32).reshape(window_rows, HK, HD)
        query_pos = row_start + query_offsets
        key_pos = row_start - W + key_offsets
        distance_back = query_pos[:, None] - key_pos[None, :]
        allowed = (distance_back >= 0) & (distance_back < W) & (key_pos[None, :] >= 0)
        scores = attn_scale * jnp.einsum("qhgd,khd->hgqk", query_block, key_block)
        scores = jnp.where(allowed, scores, -jnp.inf)
        row_max = jnp.max(scores, axis=-1, keepdims=True)
        raised = jnp.exp(scores - row_max)
        soft_weights = raised / jnp.sum(raised, axis=-1, keepdims=True)
        soft_low = lax.optimization_barrier(soft_weights.astype(jnp.bfloat16)).astype(jnp.float32)
        grad_probs = jnp.einsum("qhgd,khd->hgqk", grad_block, value_block)
        row_delta = jnp.sum(soft_weights * grad_probs, axis=-1, keepdims=True)
        grad_scores = lax.optimization_barrier((soft_weights * (grad_probs - row_delta)).astype(jnp.bfloat16)).astype(jnp.float32)
        grad_query = (attn_scale * jnp.einsum("hgqk,khd->qhgd", grad_scores, key_block)).astype(jnp.bfloat16).reshape(block_rows, HQ * HD)
        key_part = (attn_scale * jnp.einsum("hgqk,qhgd->khd", grad_scores, query_block)).reshape(window_rows, kv_width)
        value_part = jnp.einsum("hgqk,qhgd->khd", soft_low, grad_block).reshape(window_rows, kv_width)
        key_total = lax.dynamic_update_slice_in_dim(key_total, lax.dynamic_slice_in_dim(key_total, row_start, window_rows, 0) + key_part, row_start, 0)
        value_total = lax.dynamic_update_slice_in_dim(value_total, lax.dynamic_slice_in_dim(value_total, row_start, window_rows, 0) + value_part, row_start, 0)
        return (key_total, value_total), grad_query

    zero_rows = jnp.zeros((TOKENS + W, kv_width), jnp.float32)
    (key_total, value_total), grad_rows = lax.scan(one_block, (zero_rows, zero_rows), jnp.arange(TOKENS // block_rows, dtype=jnp.int32))
    query_grad = grad_rows.reshape(TOKENS, HQ * HD)
    key_low = key_total[W:].astype(jnp.bfloat16)
    value_low = value_total[W:].astype(jnp.bfloat16)
    key_weight_grad = jnp.dot(normed_input.T, key_low, preferred_element_type=jnp.float32)
    return (query_grad, key_weight_grad, value_low)
```

```python
import functools

import jax
import jax.numpy as jnp
from jax import lax
from jax.experimental import pallas as pl
from jax.experimental.pallas import tpu as pltpu
from jax.sharding import PartitionSpec as P

HD = 128
HQ = 16
HK = 8
W = 1024
GROUP = HQ // HK

attn_scale = 168.0 ** (-0.5)
log2_e = 1.4426950408889634

VMEM = pl.BlockSpec(memory_space=pltpu.VMEM)
SMEM = pl.BlockSpec(memory_space=pltpu.SMEM)
ANY = pl.BlockSpec(memory_space=pl.ANY)


def call(kernel, outs, in_specs, out_specs, scratch=(), flops=0, moved=0, name=None):
    return pl.pallas_call(
        kernel,
        out_shape=outs,
        in_specs=in_specs,
        out_specs=out_specs,
        scratch_shapes=list(scratch),
        cost_estimate=pl.CostEstimate(flops=flops, bytes_accessed=moved, transcendentals=0),
        compiler_params=pltpu.CompilerParams(vmem_limit_bytes=56 * 1024 * 1024),
        name=name,
    )


def shape(dims, kind=jnp.bfloat16):
    return jax.ShapeDtypeStruct(dims, kind)


def pack_kernel(parts, where, q_ref, k_ref, v_ref, d_ref, *outs):
    place = where[0]
    rows = q_ref.shape[0]
    full, cross = outs[:parts], outs[parts:]
    for slot in range(parts):
        head = place ^ slot
        pair = pl.ds(pl.multiple_of(head * GROUP * HD, HD), GROUP * HD)
        single = pl.ds(pl.multiple_of(head * HD, HD), HD)
        both = q_ref[:, pair]
        for g in range(GROUP):
            full[slot][g * rows : (g + 1) * rows, :] = both[:, g * HD : (g + 1) * HD]
        both = d_ref[:, pair]
        for g in range(GROUP):
            full[slot][(GROUP + g) * rows : (GROUP + g + 1) * rows, :] = both[:, g * HD : (g + 1) * HD]
        keys, values = k_ref[:, single], v_ref[:, single]
        full[slot][2 * GROUP * rows : (2 * GROUP + 1) * rows, :] = keys
        full[slot][(2 * GROUP + 1) * rows :, :] = values
        cross[slot][:rows, :] = keys
        cross[slot][rows:, :] = values


def attention_kernel(parts, rows, where, *refs):
    full, cross = refs[:parts], refs[parts : 2 * parts]
    dq_out = refs[2 * parts : 3 * parts]
    back_k, back_v, own_k, own_v = refs[3 * parts : 3 * parts + 4]
    q_s, d_s, k_s, v_s, dq_s, dk_s, dv_s, sems = refs[3 * parts + 4 :]
    place, first = where[0], where[1]
    span = parts * rows
    wide = GROUP * rows
    copies = []

    def move(source, target):
        copy = pltpu.make_async_copy(source, target, sems.at[len(copies)])
        copy.start()
        copies.append(copy)

    for slot in range(parts):
        spot = place ^ slot
        pair = pl.ds(pl.multiple_of(spot * wide, wide), wide)
        old = pl.ds(pl.multiple_of(spot * rows, rows), rows)
        new = pl.ds(pl.multiple_of(span + spot * rows, rows), rows)
        move(full[slot].at[0:wide], q_s.at[pair])
        move(full[slot].at[wide : 2 * wide], d_s.at[pair])
        move(full[slot].at[2 * wide : 2 * wide + rows], k_s.at[new])
        move(full[slot].at[2 * wide + rows : 2 * wide + 2 * rows], v_s.at[new])
        move(cross[slot].at[0:rows], k_s.at[old])
        move(cross[slot].at[rows : 2 * rows], v_s.at[old])
    dk_s[...] = jnp.zeros_like(dk_s)
    dv_s[...] = jnp.zeros_like(dv_s)
    for copy in copies:
        copy.wait()

    key_at = lax.broadcasted_iota(jnp.int32, (rows, wide), 0)
    query_at = lax.broadcasted_iota(jnp.int32, (rows, wide), 1) % rows
    older = key_at > query_at
    nt = (((1,), (1,)), ((), ()))
    chunks = parts + 1
    hidden = jnp.float32(-jnp.inf)

    def one_block(block, carry):
        pair = pl.ds(pl.multiple_of(block * wide, wide), wide)
        queries = q_s[pair, :]
        grads = d_s[pair, :]

        def keys_of(chunk):
            return pl.ds(pl.multiple_of((block + chunk) * rows, rows), rows)

        scores = []
        for chunk in range(chunks):
            s = lax.dot_general(k_s[keys_of(chunk), :], queries, nt, preferred_element_type=jnp.float32)
            s = s * (attn_scale * log2_e)
            if chunk == 0:
                s = jnp.where(older, s, hidden)
            if chunk == chunks - 1:
                s = jnp.where(older, hidden, s)
            else:
                s = s + jnp.where((first == 1) & (block + chunk < parts), hidden, 0.0)
            scores.append(s)
        top = functools.reduce(jnp.maximum, [jnp.max(s, axis=0, keepdims=True) for s in scores])
        total = jnp.zeros((1, wide), jnp.float32)
        delta = jnp.zeros((1, wide), jnp.float32)
        raised, probs = [], []
        for chunk in range(chunks):
            e = jnp.exp2(scores[chunk] - top)
            dp = lax.dot_general(v_s[keys_of(chunk), :], grads, nt, preferred_element_type=jnp.float32)
            total = total + jnp.sum(e, axis=0, keepdims=True)
            delta = delta + jnp.sum(e * dp, axis=0, keepdims=True)
            raised.append(e)
            probs.append(dp)
        inverse = 1.0 / total
        delta = delta * inverse
        dq = jnp.zeros((HD, wide), jnp.float32)
        for chunk in range(chunks):
            soft = raised[chunk] * inverse
            ds = (soft * (probs[chunk] - delta)).astype(jnp.bfloat16)
            low = soft.astype(jnp.bfloat16)
            here = keys_of(chunk)
            dv_s[here, :] += jnp.dot(low, grads, preferred_element_type=jnp.float32)
            dk_s[here, :] += jnp.dot(ds, queries, preferred_element_type=jnp.float32)
            dq += lax.dot_general(
                k_s[here, :], ds, (((0,), (0,)), ((), ())), preferred_element_type=jnp.float32
            )
        dq_s[pair, :] = (attn_scale * dq).T.astype(jnp.bfloat16)
        return carry

    lax.fori_loop(0, parts, one_block, 0)
    out_copies = []
    for slot in range(parts):
        spot = place ^ slot
        pair = pl.ds(pl.multiple_of(spot * wide, wide), wide)
        copy = pltpu.make_async_copy(dq_s.at[pair], dq_out[slot], sems.at[slot])
        copy.start()
        out_copies.append(copy)
    back_k[...] = (attn_scale * dk_s[:span, :]).astype(jnp.bfloat16)
    own_k[...] = attn_scale * dk_s[span:, :]
    back_v[...] = dv_s[:span, :].astype(jnp.bfloat16)
    own_v[...] = dv_s[span:, :]
    for copy in out_copies:
        copy.wait()


def weight_kernel(parts, rows, where, own_k, back_k, x_own, *refs):
    near, far, out = refs[: parts - 1], refs[parts - 1 : 2 * parts - 2], refs[2 * parts - 2]
    dk_s = refs[2 * parts - 1]
    place, core = where[0], where[2]
    half = rows // 2
    dk_s[...] = (own_k[...] + back_k[...].astype(jnp.float32)).astype(jnp.bfloat16)
    tt = (((0,), (0,)), ((), ()))
    spot = pl.multiple_of(place * rows, rows)
    total = lax.dot_general(dk_s[pl.ds(spot, rows), :], x_own[...], tt, preferred_element_type=jnp.float32)
    for slot in range(1, parts):
        spot = (place ^ slot) * rows
        mine = pl.ds(pl.multiple_of(spot + core * half, half), half)
        other = pl.ds(pl.multiple_of(spot + (1 - core) * half, half), half)
        total += lax.dot_general(dk_s[mine, :], near[slot - 1][...], tt, preferred_element_type=jnp.float32)
        total += lax.dot_general(dk_s[other, :], far[slot - 1][...], tt, preferred_element_type=jnp.float32)
    out[...] = total.T.astype(jnp.bfloat16)


def value_kernel(parts, rows, where, own_v, back_v, *refs):
    outs, keep = refs[:parts], refs[parts]
    keep[...] = own_v[...] + back_v[...].astype(jnp.float32)
    for slot in range(parts):
        spot = pl.multiple_of((where[0] ^ slot) * rows, rows)
        outs[slot][...] = keep[pl.ds(spot, rows), :].astype(jnp.bfloat16)


def spread_kernel(parts, width, where, *refs):
    ins, out = refs[:parts], refs[parts]
    rows = out.shape[0]
    for slot in range(parts):
        head = where[0] ^ slot
        for g in range(width):
            at = pl.ds(pl.multiple_of((head * width + g) * HD, HD), HD)
            out[:, at] = ins[slot][g * rows : (g + 1) * rows, :]


def shards(normed_input, attn_queries, attn_keys, attn_values, out_grad):
    rows, features = normed_input.shape
    heads = attn_keys.shape[1] // HD
    count = lax.axis_size("ctx")
    parts = W // rows
    assert parts == heads and count % parts == 0 and parts & (parts - 1) == 0
    blocks = count // parts
    me = lax.axis_index("ctx")
    place = me % parts
    core = lax.axis_index("tp")
    where = jnp.stack([place, (me < parts).astype(jnp.int32), core]).astype(jnp.int32)

    def within(value, slot):
        return lax.ppermute(value, "ctx", [(s, s ^ slot) for s in range(count)])

    def across(value, slot, step):
        perm = []
        for s in range(count):
            target = (s // parts + step) % blocks * parts + (s % parts ^ slot)
            perm.append((s, target))
        return lax.ppermute(value, "ctx", perm)

    wide = GROUP * rows
    span = parts * rows
    packed = call(
        functools.partial(pack_kernel, parts),
        [shape((2 * wide + 2 * rows, HD))] * parts + [shape((2 * rows, HD))] * parts,
        [SMEM] + [VMEM] * 4,
        [VMEM] * (2 * parts),
        moved=4 << 20,
        name="pack",
    )(where, attn_queries, attn_keys, attn_values, out_grad)
    full, cross = packed[:parts], packed[parts:]
    got_cross = [across(cross[slot], slot, 1) for slot in range(parts)]
    got_full = [full[0]] + [within(full[slot], slot) for slot in range(1, parts)]

    half = rows // 2
    x_half = lax.dynamic_slice_in_dim(normed_input, core * half, half, 0)
    near = [within(x_half, slot) for slot in range(1, parts)]
    far = [lax.ppermute(piece, "tp", [(0, 1), (1, 0)]) for piece in near]

    pairs = 2 * span * (parts + 1) * rows
    results = call(
        functools.partial(attention_kernel, parts, rows),
        [shape((wide, HD))] * parts
        + [shape((span, HD)), shape((span, HD)), shape((span, HD), jnp.float32), shape((span, HD), jnp.float32)],
        [SMEM] + [ANY] * (2 * parts),
        [ANY] * parts + [VMEM] * 4,
        scratch=[
            pltpu.VMEM((parts * wide, HD), jnp.bfloat16),
            pltpu.VMEM((parts * wide, HD), jnp.bfloat16),
            pltpu.VMEM((2 * span, HD), jnp.bfloat16),
            pltpu.VMEM((2 * span, HD), jnp.bfloat16),
            pltpu.VMEM((parts * wide, HD), jnp.bfloat16),
            pltpu.VMEM((2 * span, HD), jnp.float32),
            pltpu.VMEM((2 * span, HD), jnp.float32),
            pltpu.SemaphoreType.DMA((6 * parts,)),
        ],
        flops=10 * pairs * HD,
        moved=4 << 20,
        name="attention",
    )(where, *got_full, *got_cross)
    dq_parts = results[:parts]
    back_k, back_v, own_k, own_v = results[parts:]

    got_k = across(back_k, 0, -1)
    got_v = across(back_v, 0, -1)
    dq_got = [dq_parts[0]] + [within(dq_parts[slot], slot) for slot in range(1, parts)]

    partial_term = call(
        functools.partial(weight_kernel, parts, rows),
        shape((features, HD)),
        [SMEM] + [VMEM] * (2 * parts + 1),
        VMEM,
        scratch=[pltpu.VMEM((span, HD), jnp.bfloat16)],
        flops=2 * span * HD * features,
        moved=8 << 20,
        name="weight",
    )(where, own_k, got_k, normed_input, *near, *far)
    pieces = partial_term.reshape(count, features // count, HD)
    pieces = lax.all_to_all(pieces, "ctx", split_axis=0, concat_axis=0, tiled=True)
    pieces = pieces.reshape(blocks, parts, features // count, HD).astype(jnp.float32)
    weight_grad = pieces.sum(axis=0).transpose(1, 0, 2).reshape(features // count, parts * HD)

    dv_parts = call(
        functools.partial(value_kernel, parts, rows),
        [shape((rows, HD))] * parts,
        [SMEM, VMEM, VMEM],
        [VMEM] * parts,
        scratch=[pltpu.VMEM((span, HD), jnp.float32)],
        moved=1 << 20,
        name="value",
    )(where, own_v, got_v)
    dv_got = [dv_parts[0]] + [within(dv_parts[slot], slot) for slot in range(1, parts)]

    query_grad = call(
        functools.partial(spread_kernel, parts, GROUP),
        shape((rows, parts * GROUP * HD)),
        [SMEM] + [VMEM] * parts,
        VMEM,
        moved=1 << 20,
        name="spread_q",
    )(where, *dq_got)
    value_grad = call(
        functools.partial(spread_kernel, parts, 1),
        shape((rows, parts * HD)),
        [SMEM] + [VMEM] * parts,
        VMEM,
        moved=1 << 19,
        name="spread_v",
    )(where, *dv_got)
    return (query_grad, weight_grad, value_grad)


def solution(mesh):
    wide = P(("groups", "ctx"), "tp")
    return jax.shard_map(
        shards,
        mesh=mesh,
        in_specs=(P(("groups", "ctx"), None), wide, wide, wide, wide),
        out_specs=(wide, wide, wide),
        check_vma=False,
    )
```

```python
import functools

import jax
import jax.numpy as jnp
from jax import lax
from jax.experimental import pallas as pl
from jax.experimental.pallas import tpu as pltpu
from jax.sharding import PartitionSpec as P


HD = 128
HQ = 16
HK = 8
W = 1024
GROUP = HQ // HK

attn_scale = 168.0 ** (-0.5)
log2_e = 1.4426950408889634

VMEM = pl.BlockSpec(memory_space=pltpu.VMEM)
ANY = pl.BlockSpec(memory_space=pl.ANY)


def call(kernel, outs, in_specs, out_specs, scratch=(), flops=0, moved=0, room=8):
    return pl.pallas_call(
        kernel,
        out_shape=outs,
        in_specs=in_specs,
        out_specs=out_specs,
        scratch_shapes=list(scratch),
        cost_estimate=pl.CostEstimate(flops=flops, bytes_accessed=moved, transcendentals=0),
        compiler_params=pltpu.CompilerParams(vmem_limit_bytes=room << 20),
    )


def shape(dims, kind=jnp.bfloat16):
    return jax.ShapeDtypeStruct(dims, kind)


def place_of(parts):
    return lax.axis_index("ctx") % parts


def pack_kernel(parts, q_ref, k_ref, v_ref, d_ref, *outs):
    place = place_of(parts)
    rows = q_ref.shape[0]
    full, cross = outs[:parts], outs[parts:]
    for slot in range(parts):
        head = place ^ slot
        pair = pl.ds(pl.multiple_of(head * GROUP * HD, HD), GROUP * HD)
        single = pl.ds(pl.multiple_of(head * HD, HD), HD)
        both = q_ref[:, pair]
        for g in range(GROUP):
            full[slot][g * rows : (g + 1) * rows, :] = both[:, g * HD : (g + 1) * HD]
        both = d_ref[:, pair]
        for g in range(GROUP):
            full[slot][(GROUP + g) * rows : (GROUP + g + 1) * rows, :] = both[:, g * HD : (g + 1) * HD]
        keys, values = k_ref[:, single], v_ref[:, single]
        full[slot][2 * GROUP * rows : (2 * GROUP + 1) * rows, :] = keys
        full[slot][(2 * GROUP + 1) * rows :, :] = values
        cross[slot][:rows, :] = keys
        cross[slot][rows:, :] = values


def attention_kernel(parts, rows, *refs):
    full, cross = refs[:parts], refs[parts : 2 * parts]
    dq_s, back_k, back_v, own_k, own_v = refs[2 * parts : 2 * parts + 5]
    q_s, d_s, k_s, v_s, dk_s, dv_s, sems = refs[2 * parts + 5 :]
    place = place_of(parts)
    first = lax.axis_index("ctx") < parts
    span = parts * rows
    wide = GROUP * rows
    copies = []

    def move(source, target):
        copy = pltpu.make_async_copy(source, target, sems.at[len(copies)])
        copy.start()
        copies.append(copy)

    for slot in range(parts):
        spot = place ^ slot
        pair = pl.ds(pl.multiple_of(spot * wide, wide), wide)
        old = pl.ds(pl.multiple_of(spot * rows, rows), rows)
        new = pl.ds(pl.multiple_of(span + spot * rows, rows), rows)
        move(full[slot].at[0:wide], q_s.at[pair])
        move(full[slot].at[wide : 2 * wide], d_s.at[pair])
        move(full[slot].at[2 * wide : 2 * wide + rows], k_s.at[new])
        move(full[slot].at[2 * wide + rows : 2 * wide + 2 * rows], v_s.at[new])
        move(cross[slot].at[0:rows], k_s.at[old])
        move(cross[slot].at[rows : 2 * rows], v_s.at[old])
    dk_s[...] = jnp.zeros_like(dk_s)
    dv_s[...] = jnp.zeros_like(dv_s)
    for copy in copies:
        copy.wait()

    key_at = lax.broadcasted_iota(jnp.int32, (rows, wide), 0)
    query_at = lax.broadcasted_iota(jnp.int32, (rows, wide), 1) % rows
    older = key_at > query_at
    nt = (((1,), (1,)), ((), ()))
    chunks = parts + 1
    hidden = jnp.float32(-jnp.inf)

    def one_block(block, carry):
        pair = pl.ds(pl.multiple_of(block * wide, wide), wide)
        queries = q_s[pair, :]
        grads = d_s[pair, :]

        def keys_of(chunk):
            return pl.ds(pl.multiple_of((block + chunk) * rows, rows), rows)

        scores = []
        for chunk in range(chunks):
            s = lax.dot_general(k_s[keys_of(chunk), :], queries, nt, preferred_element_type=jnp.float32)
            s = s * (attn_scale * log2_e)
            if chunk == 0:
                s = jnp.where(older, s, hidden)
            if chunk == chunks - 1:
                s = jnp.where(older, hidden, s)
            else:
                s = s + jnp.where(first & (block + chunk < parts), hidden, 0.0)
            scores.append(s)
        top = functools.reduce(jnp.maximum, [jnp.max(s, axis=0, keepdims=True) for s in scores])
        total = jnp.zeros((1, wide), jnp.float32)
        delta = jnp.zeros((1, wide), jnp.float32)
        raised, probs = [], []
        for chunk in range(chunks):
            e = jnp.exp2(scores[chunk] - top)
            dp = lax.dot_general(v_s[keys_of(chunk), :], grads, nt, preferred_element_type=jnp.float32)
            total = total + jnp.sum(e, axis=0, keepdims=True)
            delta = delta + jnp.sum(e * dp, axis=0, keepdims=True)
            raised.append(e)
            probs.append(dp)
        inverse = 1.0 / total
        delta = delta * inverse
        dq = jnp.zeros((HD, wide), jnp.float32)
        for chunk in range(chunks):
            soft = raised[chunk] * inverse
            ds = (soft * (probs[chunk] - delta)).astype(jnp.bfloat16)
            low = soft.astype(jnp.bfloat16)
            here = keys_of(chunk)
            dv_s[here, :] += jnp.dot(low, grads, preferred_element_type=jnp.float32)
            dk_s[here, :] += jnp.dot(ds, queries, preferred_element_type=jnp.float32)
            dq += lax.dot_general(
                k_s[here, :], ds, (((0,), (0,)), ((), ())), preferred_element_type=jnp.float32
            )
        dq_s[pair, :] = (attn_scale * dq).T.astype(jnp.bfloat16)
        return carry

    lax.fori_loop(0, parts, one_block, 0)
    back_k[...] = (attn_scale * dk_s[:span, :]).astype(jnp.bfloat16)
    own_k[...] = attn_scale * dk_s[span:, :]
    back_v[...] = dv_s[:span, :].astype(jnp.bfloat16)
    own_v[...] = dv_s[span:, :]


def weight_kernel(parts, count, rows, own_k, back_k, x_own, *refs):
    near, far = refs[: parts - 1], refs[parts - 1 : 2 * parts - 2]
    outs = refs[2 * parts - 2 : -4]
    dk_s, x_s, w_s, sems = refs[-4:]
    place, core = place_of(parts), lax.axis_index("tp")
    half = rows // 2
    copies = []

    def move(source, at, size):
        target = x_s.at[pl.ds(pl.multiple_of(at, half), size)]
        copy = pltpu.make_async_copy(source, target, sems.at[len(copies)])
        copy.start()
        copies.append(copy)

    move(x_own, place * rows, rows)
    for slot in range(1, parts):
        spot = (place ^ slot) * rows
        move(near[slot - 1], spot + core * half, half)
        move(far[slot - 1], spot + (1 - core) * half, half)
    dk_s[...] = (own_k[...] + back_k[...].astype(jnp.float32)).astype(jnp.bfloat16).T
    for copy in copies:
        copy.wait()
    total = jnp.dot(dk_s[...], x_s[...], preferred_element_type=jnp.float32)
    if len(outs) == 1:
        outs[0][...] = total.T.astype(jnp.bfloat16)
        return
    w_s[...] = total.T.astype(jnp.bfloat16)
    piece = w_s.shape[0] // count
    for slot in range(count):
        at = (lax.axis_index("ctx") ^ slot) * piece
        outs[slot][...] = w_s[pl.ds(pl.multiple_of(at, 16), piece), :]


def gather_kernel(parts, *refs):
    ins, out = refs[:-1], refs[-1]
    for slot in range(parts):
        at = pl.ds(pl.multiple_of((place_of(parts) ^ slot) * HD, HD), HD)
        out[:, at] = ins[slot][...].astype(jnp.float32) + ins[slot + parts][...].astype(jnp.float32)


def value_kernel(parts, rows, dq, own_v, back_v, *outs):
    wide = GROUP * rows
    for slot in range(parts):
        spot = place_of(parts) ^ slot
        outs[slot][:wide, :] = dq[pl.ds(pl.multiple_of(spot * wide, wide), wide), :]
        at = pl.ds(pl.multiple_of(spot * rows, rows), rows)
        outs[slot][wide:, :] = (own_v[at, :] + back_v[at, :].astype(jnp.float32)).astype(jnp.bfloat16)


def spread_kernel(parts, *refs):
    ins, dq_out, dv_out = refs[:parts], refs[-2], refs[-1]
    rows = dq_out.shape[0]
    for slot in range(parts):
        head = place_of(parts) ^ slot
        for g in range(GROUP):
            at = pl.ds(pl.multiple_of((head * GROUP + g) * HD, HD), HD)
            dq_out[:, at] = ins[slot][g * rows : (g + 1) * rows, :]
        dv_out[:, pl.ds(pl.multiple_of(head * HD, HD), HD)] = ins[slot][GROUP * rows :, :]


def shards(normed_input, attn_queries, attn_keys, attn_values, out_grad):
    rows, features = normed_input.shape
    heads = attn_keys.shape[1] // HD
    count = lax.axis_size("ctx")
    parts = W // rows
    assert parts == heads and count % parts == 0 and parts & (parts - 1) == 0
    blocks = count // parts
    core = lax.axis_index("tp")

    def within(value, slot):
        return lax.ppermute(value, "ctx", [(s, s ^ slot) for s in range(count)])

    def across(value, slot, step):
        perm = []
        for s in range(count):
            target = (s // parts + step) * parts + (s % parts ^ slot)
            if 0 <= target < count:
                perm.append((s, target))
        return lax.ppermute(value, "ctx", perm)

    def swapped(value):
        return lax.ppermute(value, "tp", [(0, 1), (1, 0)])

    wide = GROUP * rows
    span = parts * rows
    packed = call(
        functools.partial(pack_kernel, parts),
        [shape((2 * wide + 2 * rows, HD))] * parts + [shape((2 * rows, HD))] * parts,
        [VMEM] * 4,
        [VMEM] * (2 * parts),
        moved=4 << 20,
        room=56,
    )(attn_queries, attn_keys, attn_values, out_grad)
    full, cross = packed[:parts], packed[parts:]
    got_cross = [across(cross[slot], slot, 1) for slot in range(parts)]
    got_full = [full[0]] + [within(full[slot], slot) for slot in range(1, parts)]

    half = rows // 2
    x_half = lax.dynamic_slice_in_dim(normed_input, core * half, half, 0)
    near = [within(x_half, slot) for slot in range(1, parts)]
    far = [swapped(piece) for piece in near]

    pairs = 2 * span * (parts + 1) * rows
    results = call(
        functools.partial(attention_kernel, parts, rows),
        [shape((parts * wide, HD)), shape((span, HD)), shape((span, HD))]
        + [shape((span, HD), jnp.float32)] * 2,
        [ANY] * (2 * parts),
        [VMEM] * 5,
        scratch=[
            pltpu.VMEM((parts * wide, HD), jnp.bfloat16),
            pltpu.VMEM((parts * wide, HD), jnp.bfloat16),
            pltpu.VMEM((2 * span, HD), jnp.bfloat16),
            pltpu.VMEM((2 * span, HD), jnp.bfloat16),
            pltpu.VMEM((2 * span, HD), jnp.float32),
            pltpu.VMEM((2 * span, HD), jnp.float32),
            pltpu.SemaphoreType.DMA((6 * parts,)),
        ],
        flops=10 * pairs * HD,
        moved=4 << 20,
        room=32,
    )(*got_full, *got_cross)
    dq, back_k, back_v, own_k, own_v = results
    got_k = across(back_k, 0, -1)
    got_v = across(back_v, 0, -1)
    mine = call(
        functools.partial(value_kernel, parts, rows),
        [shape((wide + rows, HD))] * parts,
        [VMEM] * 3,
        [VMEM] * parts,
        moved=1 << 20,
    )(dq, own_v, got_v)
    got_mine = [mine[0]] + [within(mine[slot], slot) for slot in range(1, parts)]

    piece = features // count
    direct = blocks == 2
    terms = call(
        functools.partial(weight_kernel, parts, count, rows),
        [shape((piece, HD))] * count if direct else [shape((features, HD))],
        [VMEM] * 2 + [ANY] * (2 * parts - 1),
        [VMEM] * (count if direct else 1),
        scratch=[
            pltpu.VMEM((HD, span), jnp.bfloat16),
            pltpu.VMEM((span, features), jnp.bfloat16),
            pltpu.VMEM((features, HD), jnp.bfloat16),
            pltpu.SemaphoreType.DMA((2 * parts - 1,)),
        ],
        flops=2 * span * HD * features,
        moved=8 << 20,
        room=24,
    )(own_k, got_k, normed_input, *near, *far)
    if direct:
        got_w = [terms[0]] + [within(terms[slot], slot) for slot in range(1, count)]
        weight_grad = call(
            functools.partial(gather_kernel, parts),
            shape((piece, parts * HD), jnp.float32),
            [VMEM] * count,
            VMEM,
            moved=2 << 20,
        )(*got_w)
    else:
        pieces = terms[0].reshape(count, piece, HD)
        pieces = lax.all_to_all(pieces, "ctx", split_axis=0, concat_axis=0, tiled=True)
        pieces = pieces.reshape(blocks, parts, piece, HD).astype(jnp.float32)
        weight_grad = pieces.sum(axis=0).transpose(1, 0, 2).reshape(piece, parts * HD)

    query_grad, value_grad = call(
        functools.partial(spread_kernel, parts),
        [shape((rows, parts * GROUP * HD)), shape((rows, parts * HD))],
        [VMEM] * parts,
        [VMEM] * 2,
        moved=2 << 20,
    )(*got_mine)
    return (query_grad, weight_grad, value_grad)


def solution(mesh):
    wide = P(("groups", "ctx"), "tp")

    return jax.shard_map(
        shards,
        mesh=mesh,
        in_specs=(P(("groups", "ctx"), None), wide, wide, wide, wide),
        out_specs=(wide, wide, wide),
        check_vma=False,
    )
```

```python
import functools

import jax
import jax.numpy as jnp
from jax import lax
from jax.experimental import pallas as pl
from jax.experimental.pallas import tpu as pltpu
from jax.sharding import PartitionSpec as P


HD = 128
HQ = 16
HK = 8
W = 1024
GROUP = HQ // HK

attn_scale = 168.0 ** (-0.5)
log2_e = 1.4426950408889634

VMEM = pl.BlockSpec(memory_space=pltpu.VMEM)
ANY = pl.BlockSpec(memory_space=pl.ANY)


def call(kernel, outs, in_specs, out_specs, scratch=(), flops=0, moved=0, room=8):
    return pl.pallas_call(
        kernel,
        out_shape=outs,
        in_specs=in_specs,
        out_specs=out_specs,
        scratch_shapes=list(scratch),
        cost_estimate=pl.CostEstimate(flops=flops, bytes_accessed=moved, transcendentals=0),
        compiler_params=pltpu.CompilerParams(vmem_limit_bytes=room << 20),
    )


def shape(dims, kind=jnp.bfloat16):
    return jax.ShapeDtypeStruct(dims, kind)


def place_of(parts):
    return lax.axis_index("ctx") % parts


def pack_kernel(parts, slots, crosses, q_ref, k_ref, v_ref, d_ref, *refs):
    count = len(slots) + crosses
    outs, held, sems, out_sems = refs[:count], refs[count : 2 * count], refs[-2], refs[-1]
    rows = q_ref.shape[0]
    copies = []
    for at in range(count):
        cross = at >= len(slots)
        head = place_of(parts) ^ (at - len(slots) if cross else slots[at])
        sources = [(k_ref, head), (v_ref, head)]
        if not cross:
            sources = [(ref, head * GROUP + g) for ref in (q_ref, d_ref) for g in range(GROUP)] + sources
        mine = []
        for step, (ref, column) in enumerate(sources):
            source = ref.at[:, pl.ds(pl.multiple_of(column * HD, HD), HD)]
            target = held[at].at[step * rows : (step + 1) * rows]
            copy = pltpu.make_async_copy(source, target, sems.at[at, step])
            copy.start()
            mine.append(copy)
        copies.append(mine)
    sent = []
    for at, mine in enumerate(copies):
        for copy in mine:
            copy.wait()
        copy = pltpu.make_async_copy(held[at], outs[at], out_sems.at[at])
        copy.start()
        sent.append(copy)
    for copy in sent:
        copy.wait()


def attention_kernel(parts, rows, *refs):
    full, cross = refs[:parts], refs[parts : 2 * parts]
    dq_s, back_k, back_v, own_k, own_v = refs[2 * parts : 2 * parts + 5]
    q_s, d_s, k_s, v_s, dk_s, dv_s, sems = refs[2 * parts + 5 :]
    place = place_of(parts)
    first = lax.axis_index("ctx") < parts
    span = parts * rows
    wide = GROUP * rows
    copies = []

    def move(source, target):
        copy = pltpu.make_async_copy(source, target, sems.at[len(copies)])
        copy.start()
        copies.append(copy)

    for slot in range(parts):
        spot = place ^ slot
        pair = pl.ds(pl.multiple_of(spot * wide, wide), wide)
        old = pl.ds(pl.multiple_of(spot * rows, rows), rows)
        new = pl.ds(pl.multiple_of(span + spot * rows, rows), rows)
        move(full[slot].at[0:wide], q_s.at[pair])
        move(full[slot].at[wide : 2 * wide], d_s.at[pair])
        move(full[slot].at[2 * wide : 2 * wide + rows], k_s.at[new])
        move(full[slot].at[2 * wide + rows : 2 * wide + 2 * rows], v_s.at[new])
        move(cross[slot].at[0:rows], k_s.at[old])
        move(cross[slot].at[rows : 2 * rows], v_s.at[old])
    dk_s[...] = jnp.zeros_like(dk_s)
    dv_s[...] = jnp.zeros_like(dv_s)
    for copy in copies:
        copy.wait()

    key_at = lax.broadcasted_iota(jnp.int32, (rows, wide), 0)
    query_at = lax.broadcasted_iota(jnp.int32, (rows, wide), 1) % rows
    older = key_at > query_at
    nt = (((1,), (1,)), ((), ()))
    chunks = parts + 1
    hidden = jnp.float32(-jnp.inf)

    def one_block(block, skipped):
        pair = slice(block * wide, (block + 1) * wide)
        queries = q_s[pair, :]
        grads = d_s[pair, :]

        def keys_of(chunk):
            return slice((block + chunk) * rows, (block + chunk + 1) * rows)

        used = [chunk for chunk in range(chunks) if block + chunk >= skipped]
        scores = {}
        for chunk in used:
            s = lax.dot_general(k_s[keys_of(chunk), :], queries, nt, preferred_element_type=jnp.float32)
            s = s * (attn_scale * log2_e)
            if chunk == 0:
                s = jnp.where(older, s, hidden)
            if chunk == chunks - 1:
                s = jnp.where(older, hidden, s)
            scores[chunk] = s
        top = functools.reduce(jnp.maximum, [jnp.max(s, axis=0, keepdims=True) for s in scores.values()])
        total = jnp.zeros((1, wide), jnp.float32)
        delta = jnp.zeros((1, wide), jnp.float32)
        raised, probs = {}, {}
        for chunk in used:
            e = jnp.exp2(scores[chunk] - top)
            dp = lax.dot_general(v_s[keys_of(chunk), :], grads, nt, preferred_element_type=jnp.float32)
            total = total + jnp.sum(e, axis=0, keepdims=True)
            delta = delta + jnp.sum(e * dp, axis=0, keepdims=True)
            raised[chunk] = e
            probs[chunk] = dp
        inverse = 1.0 / total
        delta = delta * inverse
        dq = jnp.zeros((HD, wide), jnp.float32)
        for chunk in used:
            soft = raised[chunk] * inverse
            ds = (soft * (probs[chunk] - delta)).astype(jnp.bfloat16)
            low = soft.astype(jnp.bfloat16)
            here = keys_of(chunk)
            dv_s[here, :] += jnp.dot(low, grads, preferred_element_type=jnp.float32)
            dk_s[here, :] += jnp.dot(ds, queries, preferred_element_type=jnp.float32)
            dq += lax.dot_general(
                k_s[here, :], ds, (((0,), (0,)), ((), ())), preferred_element_type=jnp.float32
            )
        dq_s[pair, :] = (attn_scale * dq).T.astype(jnp.bfloat16)

    for skipped, here in ((parts, first), (0, jnp.logical_not(first))):

        @pl.when(here)
        def _(skipped=skipped):
            for block in range(parts):
                one_block(block, skipped)

    back_k[...] = (attn_scale * dk_s[:span, :]).astype(jnp.bfloat16)
    own_k[...] = attn_scale * dk_s[span:, :]
    back_v[...] = dv_s[:span, :].astype(jnp.bfloat16)
    own_v[...] = dv_s[span:, :]


def weight_kernel(parts, count, rows, spots, own_k, back_k, x_own, *refs):
    pieces, outs = refs[: 2 * len(spots)], refs[2 * len(spots) : -4]
    dk_s, x_s, w_s, sems = refs[-4:]
    place, core = place_of(parts), lax.axis_index("tp")
    half = rows // 2
    copies = []

    def move(source, at):
        target = x_s.at[pl.ds(pl.multiple_of(at, 64), source.shape[0])]
        copy = pltpu.make_async_copy(source, target, sems.at[len(copies)])
        copy.start()
        copies.append(copy)

    move(x_own, place * rows)
    for at, (slot, offset) in enumerate(spots):
        base = (place ^ slot) * rows + offset
        move(pieces[2 * at], base + core * half)
        move(pieces[2 * at + 1], base + (1 - core) * half)
    dk_s[...] = (own_k[...] + back_k[...].astype(jnp.float32)).astype(jnp.bfloat16).T
    for copy in copies:
        copy.wait()
    total = jnp.dot(dk_s[...], x_s[...], preferred_element_type=jnp.float32)
    if len(outs) == 1:
        outs[0][...] = total.T.astype(jnp.bfloat16)
        return
    w_s[...] = total.T.astype(jnp.bfloat16)
    piece = w_s.shape[0] // count
    for slot in range(count):
        at = (lax.axis_index("ctx") ^ slot) * piece
        outs[slot][...] = w_s[pl.ds(pl.multiple_of(at, 16), piece), :]


def split_kernel(parts, rows, value, *outs):
    for slot in range(parts):
        at = (place_of(parts) ^ slot) * rows
        outs[slot][...] = value[pl.ds(pl.multiple_of(at, rows), rows), :]


def value_kernel(parts, rows, own_v, back_v, *outs):
    for slot in range(parts):
        at = pl.ds(pl.multiple_of((place_of(parts) ^ slot) * rows, rows), rows)
        outs[slot][...] = (own_v[at, :] + back_v[at, :].astype(jnp.float32)).astype(jnp.bfloat16)


def spread_kernel(parts, *refs):
    dq, dv = refs[:parts], refs[parts : 2 * parts]
    outs = refs[-3:] if len(refs) > 2 * parts + 2 else refs[-2:]
    terms = refs[2 * parts : -len(outs)]
    rows = outs[0].shape[0]
    for slot in range(parts):
        head = place_of(parts) ^ slot
        for g in range(GROUP):
            at = pl.ds(pl.multiple_of((head * GROUP + g) * HD, HD), HD)
            outs[0][:, at] = dq[slot][g * rows : (g + 1) * rows, :]
        at = pl.ds(pl.multiple_of(head * HD, HD), HD)
        outs[1][:, at] = dv[slot][...]
        if terms:
            outs[2][:, at] = terms[slot][...].astype(jnp.float32) + terms[slot + parts][...].astype(jnp.float32)


def shards(normed_input, attn_queries, attn_keys, attn_values, out_grad):
    rows, features = normed_input.shape
    heads = attn_keys.shape[1] // HD
    count = lax.axis_size("ctx")
    parts = W // rows
    assert parts == heads and count % parts == 0 and parts & (parts - 1) == 0
    blocks = count // parts
    core = lax.axis_index("tp")

    def within(value, slot):
        return lax.ppermute(value, "ctx", [(s, s ^ slot) for s in range(count)])

    def across(value, slot, step):
        perm = []
        for s in range(count):
            target = (s // parts + step) * parts + (s % parts ^ slot)
            if 0 <= target < count:
                perm.append((s, target))
        return lax.ppermute(value, "ctx", perm)

    def swapped(value):
        return lax.ppermute(value, "tp", [(0, 1), (1, 0)])

    wide = GROUP * rows
    span = parts * rows

    def pack(slots, crosses):
        shapes = [(2 * wide + 2 * rows, HD)] * len(slots) + [(2 * rows, HD)] * crosses
        return call(
            functools.partial(pack_kernel, parts, slots, crosses),
            [shape(dims) for dims in shapes],
            [ANY] * 4,
            [ANY] * len(shapes),
            scratch=[pltpu.VMEM(dims, jnp.bfloat16) for dims in shapes]
            + [pltpu.SemaphoreType.DMA((len(shapes), 2 * GROUP + 2)), pltpu.SemaphoreType.DMA((len(shapes),))],
            moved=2 << 20,
            room=56,
        )(attn_queries, attn_keys, attn_values, out_grad)

    full_2, full_3, full_1, full_0, *cross = pack((2, 3, 1, 0), parts)
    full = (full_0, full_1, full_2, full_3)
    got_cross = [across(cross[slot], slot, 1) for slot in range(parts)]
    got_full = [full[0]] + [within(full[slot], slot) for slot in range(1, parts)]

    half = rows // 2
    x_half = lax.dynamic_slice_in_dim(normed_input, core * half, half, 0)
    quarter = half // 2
    near_2 = within(x_half, 2)
    near_3 = within(x_half[:quarter], 3)
    near_1 = within(x_half, 1)
    relay = within(near_2[quarter:], 1)
    spots = ((2, 0), (3, 0), (1, 0), (3, quarter))
    x_pieces = []
    for piece in (near_2, near_3, near_1, relay):
        x_pieces += [piece, swapped(piece)]

    pairs = 2 * span * (parts + 1) * rows
    results = call(
        functools.partial(attention_kernel, parts, rows),
        [shape((parts * wide, HD)), shape((span, HD)), shape((span, HD))]
        + [shape((span, HD), jnp.float32)] * 2,
        [ANY] * (2 * parts),
        [VMEM] * 5,
        scratch=[
            pltpu.VMEM((parts * wide, HD), jnp.bfloat16),
            pltpu.VMEM((parts * wide, HD), jnp.bfloat16),
            pltpu.VMEM((2 * span, HD), jnp.bfloat16),
            pltpu.VMEM((2 * span, HD), jnp.bfloat16),
            pltpu.VMEM((2 * span, HD), jnp.float32),
            pltpu.VMEM((2 * span, HD), jnp.float32),
            pltpu.SemaphoreType.DMA((6 * parts,)),
        ],
        flops=10 * pairs * HD,
        moved=4 << 20,
        room=32,
    )(*got_full, *got_cross)
    dq, back_k, back_v, own_k, own_v = results
    got_k = across(back_k, 0, -1)
    got_v = across(back_v, 0, -1)

    def exchanged(values):
        return [values[0]] + [within(values[slot], slot) for slot in range(1, parts)]

    dq_parts = call(
        functools.partial(split_kernel, parts, wide), [shape((wide, HD))] * parts, [VMEM], [VMEM] * parts, moved=1 << 20
    )(dq)
    got_dq = exchanged(dq_parts)
    dv_parts = call(
        functools.partial(value_kernel, parts, rows),
        [shape((rows, HD))] * parts,
        [VMEM] * 2,
        [VMEM] * parts,
        moved=1 << 20,
    )(own_v, got_v)
    got_dv = exchanged(dv_parts)

    piece = features // count
    direct = blocks == 2
    terms = call(
        functools.partial(weight_kernel, parts, count, rows, spots),
        [shape((piece, HD))] * count if direct else [shape((features, HD))],
        [VMEM] * 2 + [ANY] * (1 + len(x_pieces)),
        [VMEM] * (count if direct else 1),
        scratch=[
            pltpu.VMEM((HD, span), jnp.bfloat16),
            pltpu.VMEM((span, features), jnp.bfloat16),
            pltpu.VMEM((features, HD), jnp.bfloat16),
            pltpu.SemaphoreType.DMA((1 + len(x_pieces),)),
        ],
        flops=2 * span * HD * features,
        moved=8 << 20,
        room=24,
    )(own_k, got_k, normed_input, *x_pieces)
    got_terms = []
    if direct:
        got_terms = [terms[0]] + [within(terms[slot], slot) for slot in range(1, count)]

    outs = call(
        functools.partial(spread_kernel, parts),
        [shape((rows, parts * GROUP * HD)), shape((rows, parts * HD))]
        + ([shape((piece, parts * HD), jnp.float32)] if direct else []),
        [VMEM] * (2 * parts + len(got_terms)),
        [VMEM] * (3 if direct else 2),
        moved=3 << 20,
    )(*got_dq, *got_dv, *got_terms)
    query_grad, value_grad = outs[:2]
    if direct:
        weight_grad = outs[2]
    else:
        pieces = terms[0].reshape(count, piece, HD)
        pieces = lax.all_to_all(pieces, "ctx", split_axis=0, concat_axis=0, tiled=True)
        pieces = pieces.reshape(blocks, parts, piece, HD).astype(jnp.float32)
        weight_grad = pieces.sum(axis=0).transpose(1, 0, 2).reshape(piece, parts * HD)
    return (query_grad, weight_grad, value_grad)


def solution(mesh):
    wide = P(("groups", "ctx"), "tp")

    return jax.shard_map(
        shards,
        mesh=mesh,
        in_specs=(P(("groups", "ctx"), None), wide, wide, wide, wide),
        out_specs=(wide, wide, wide),
        check_vma=False,
    )
```

```python
import functools

import jax
import jax.numpy as jnp
from jax import lax
from jax.experimental import pallas as pl
from jax.experimental.pallas import tpu as pltpu
from jax.sharding import PartitionSpec as P


HD = 128
HQ = 16
HK = 8
W = 1024
GROUP = HQ // HK

attn_scale = 168.0 ** (-0.5)
log2_e = 1.4426950408889634

VMEM = pl.BlockSpec(memory_space=pltpu.VMEM)
ANY = pl.BlockSpec(memory_space=pl.ANY)


def call(kernel, outs, in_specs, out_specs, scratch=(), flops=0, moved=0, room=8):
    return pl.pallas_call(
        kernel,
        out_shape=outs,
        in_specs=in_specs,
        out_specs=out_specs,
        scratch_shapes=list(scratch),
        cost_estimate=pl.CostEstimate(flops=flops, bytes_accessed=moved, transcendentals=0),
        compiler_params=pltpu.CompilerParams(vmem_limit_bytes=room << 20),
    )


def shape(dims, kind=jnp.bfloat16):
    return jax.ShapeDtypeStruct(dims, kind)


def place_of(parts):
    return lax.axis_index("ctx") % parts


def pack_kernel(parts, slots, crosses, q_ref, k_ref, v_ref, d_ref, *refs):
    count = len(slots) + crosses
    outs, held, sems, out_sems = refs[:count], refs[count : 2 * count], refs[-2], refs[-1]
    rows = q_ref.shape[0]
    copies = []
    for at in range(count):
        cross = at >= len(slots)
        head = place_of(parts) ^ (at - len(slots) if cross else slots[at])
        sources = [(k_ref, head), (v_ref, head)]
        if not cross:
            sources = [(ref, head * GROUP + g) for ref in (q_ref, d_ref) for g in range(GROUP)] + sources
        mine = []
        for step, (ref, column) in enumerate(sources):
            source = ref.at[:, pl.ds(pl.multiple_of(column * HD, HD), HD)]
            target = held[at].at[step * rows : (step + 1) * rows]
            copy = pltpu.make_async_copy(source, target, sems.at[at, step])
            copy.start()
            mine.append(copy)
        copies.append(mine)
    sent = []
    for at, mine in enumerate(copies):
        for copy in mine:
            copy.wait()
        copy = pltpu.make_async_copy(held[at], outs[at], out_sems.at[at])
        copy.start()
        sent.append(copy)
    for copy in sent:
        copy.wait()


def attention_kernel(parts, rows, *refs):
    full, cross = refs[:parts], refs[parts : 2 * parts]
    dq_s, back_k, back_v, own_k, own_v = refs[2 * parts : 2 * parts + 5]
    q_s, d_s, k_s, v_s, dk_s, dv_s, s_s, p_s, sems = refs[2 * parts + 5 :]
    place = place_of(parts)
    first = lax.axis_index("ctx") < parts
    span = parts * rows
    wide = GROUP * rows
    copies = []

    def move(source, target):
        copy = pltpu.make_async_copy(source, target, sems.at[len(copies)])
        copy.start()
        copies.append(copy)

    for slot in range(parts):
        spot = place ^ slot
        pair = pl.ds(pl.multiple_of(spot * wide, wide), wide)
        old = pl.ds(pl.multiple_of(spot * rows, rows), rows)
        new = pl.ds(pl.multiple_of(span + spot * rows, rows), rows)
        move(full[slot].at[0:wide], q_s.at[pair])
        move(full[slot].at[wide : 2 * wide], d_s.at[pair])
        move(full[slot].at[2 * wide : 2 * wide + rows], k_s.at[new])
        move(full[slot].at[2 * wide + rows : 2 * wide + 2 * rows], v_s.at[new])
        move(cross[slot].at[0:rows], k_s.at[old])
        move(cross[slot].at[rows : 2 * rows], v_s.at[old])
    dk_s[...] = jnp.zeros_like(dk_s)
    dv_s[...] = jnp.zeros_like(dv_s)
    for copy in copies:
        copy.wait()

    key_at = lax.broadcasted_iota(jnp.int32, (rows, rows), 0)
    older = key_at > lax.broadcasted_iota(jnp.int32, (rows, rows), 1)
    nt = (((1,), (1,)), ((), ()))
    chunks = parts + 1
    hidden = jnp.float32(-jnp.inf)

    def queries_of(task):
        at = (task // GROUP) * wide + (task % GROUP) * rows
        return slice(at, at + rows)

    def keys_of(task, chunk):
        at = (task // GROUP + chunk) * rows
        return slice(at, at + rows)

    def held(chunk):
        return slice(chunk * rows, (chunk + 1) * rows)

    def scores(task, chunk):
        keys, slot = keys_of(task, chunk), task % 2
        s = lax.dot_general(k_s[keys, :], q_s[queries_of(task), :], nt, preferred_element_type=jnp.float32)
        s = s * (attn_scale * log2_e)
        if chunk == 0:
            s = jnp.where(older, s, hidden)
        if chunk == chunks - 1:
            s = jnp.where(older, hidden, s)
        s_s[slot, held(chunk), :] = s
        p_s[slot, held(chunk), :] = lax.dot_general(
            v_s[keys, :], d_s[queries_of(task), :], nt, preferred_element_type=jnp.float32
        )
        return jnp.max(s, axis=0, keepdims=True)

    def all_tasks(skipped):
        count = parts * GROUP

        def used(task):
            return [chunk for chunk in range(chunks) if task // GROUP + chunk >= skipped]

        top = functools.reduce(jnp.maximum, [scores(0, chunk) for chunk in used(0)])
        for task in range(count):
            slot = task % 2
            total = jnp.zeros((1, rows), jnp.float32)
            delta = jnp.zeros((1, rows), jnp.float32)
            tops = []
            following = list(used(task + 1)) if task + 1 < count else []
            for chunk in used(task):
                e = jnp.exp2(s_s[slot, held(chunk), :] - top)
                s_s[slot, held(chunk), :] = e
                total = total + jnp.sum(e, axis=0, keepdims=True)
                delta = delta + jnp.sum(e * p_s[slot, held(chunk), :], axis=0, keepdims=True)
                if following:
                    tops.append(scores(task + 1, following.pop(0)))
            inverse = 1.0 / total
            delta = delta * inverse
            dq = jnp.zeros((HD, rows), jnp.float32)
            for chunk in used(task):
                soft = s_s[slot, held(chunk), :] * inverse
                ds = (soft * (p_s[slot, held(chunk), :] - delta)).astype(jnp.bfloat16)
                low = soft.astype(jnp.bfloat16)
                here = keys_of(task, chunk)
                dv_s[here, :] += jnp.dot(low, d_s[queries_of(task), :], preferred_element_type=jnp.float32)
                dk_s[here, :] += jnp.dot(ds, q_s[queries_of(task), :], preferred_element_type=jnp.float32)
                dq += lax.dot_general(
                    k_s[here, :], ds, (((0,), (0,)), ((), ())), preferred_element_type=jnp.float32
                )
                if following:
                    tops.append(scores(task + 1, following.pop(0)))
            dq_s[queries_of(task), :] = (attn_scale * dq).T.astype(jnp.bfloat16)
            while following:
                tops.append(scores(task + 1, following.pop(0)))
            if tops:
                top = functools.reduce(jnp.maximum, tops)

    for skipped, here in ((parts, first), (0, jnp.logical_not(first))):

        @pl.when(here)
        def _(skipped=skipped):
            all_tasks(skipped)

    back_k[...] = (attn_scale * dk_s[:span, :]).astype(jnp.bfloat16)
    own_k[...] = attn_scale * dk_s[span:, :]
    back_v[...] = dv_s[:span, :].astype(jnp.bfloat16)
    own_v[...] = dv_s[span:, :]


def weight_kernel(parts, count, rows, spots, own_k, back_k, x_own, *refs):
    pieces, outs = refs[: 2 * len(spots)], refs[2 * len(spots) : -4]
    dk_s, x_s, w_s, sems = refs[-4:]
    place, core = place_of(parts), lax.axis_index("tp")
    half = rows // 2
    copies = []

    def move(source, at):
        target = x_s.at[pl.ds(pl.multiple_of(at, 64), source.shape[0])]
        copy = pltpu.make_async_copy(source, target, sems.at[len(copies)])
        copy.start()
        copies.append(copy)

    move(x_own, place * rows)
    for at, (slot, offset) in enumerate(spots):
        base = (place ^ slot) * rows + offset
        move(pieces[2 * at], base + core * half)
        move(pieces[2 * at + 1], base + (1 - core) * half)
    dk_s[...] = (own_k[...] + back_k[...].astype(jnp.float32)).astype(jnp.bfloat16).T
    for copy in copies:
        copy.wait()
    total = jnp.dot(dk_s[...], x_s[...], preferred_element_type=jnp.float32)
    if len(outs) == 1:
        outs[0][...] = total.T.astype(jnp.bfloat16)
        return
    w_s[...] = total.T.astype(jnp.bfloat16)
    piece = w_s.shape[0] // count
    for slot in range(count):
        at = (lax.axis_index("ctx") ^ slot) * piece
        outs[slot][...] = w_s[pl.ds(pl.multiple_of(at, 16), piece), :]


def split_kernel(parts, rows, value, *outs):
    for slot in range(parts):
        at = (place_of(parts) ^ slot) * rows
        outs[slot][...] = value[pl.ds(pl.multiple_of(at, rows), rows), :]


def value_kernel(parts, rows, own_v, back_v, *refs):
    terms, outs = refs[:-parts], refs[-parts:]
    for slot in range(parts):
        at = pl.ds(pl.multiple_of((place_of(parts) ^ slot) * rows, rows), rows)
        outs[slot][:rows, :] = (own_v[at, :] + back_v[at, :].astype(jnp.float32)).astype(jnp.bfloat16)
        if terms:
            outs[slot][rows:, :] = terms[slot][...]


def spread_kernel(parts, *refs):
    dq, dv = refs[:parts], refs[parts : 2 * parts]
    outs = refs[-3:] if len(refs) > 2 * parts + 2 else refs[-2:]
    terms = refs[2 * parts : -len(outs)]
    rows = outs[0].shape[0]
    for slot in range(parts):
        head = place_of(parts) ^ slot
        for g in range(GROUP):
            at = pl.ds(pl.multiple_of((head * GROUP + g) * HD, HD), HD)
            outs[0][:, at] = dq[slot][g * rows : (g + 1) * rows, :]
        at = pl.ds(pl.multiple_of(head * HD, HD), HD)
        outs[1][:, at] = dv[slot][:rows, :]
        if terms:
            outs[2][:, at] = dv[slot][rows:, :].astype(jnp.float32) + terms[slot][...].astype(jnp.float32)


def shards(normed_input, attn_queries, attn_keys, attn_values, out_grad):
    rows, features = normed_input.shape
    heads = attn_keys.shape[1] // HD
    count = lax.axis_size("ctx")
    parts = W // rows
    assert parts == heads and count % parts == 0 and parts & (parts - 1) == 0
    blocks = count // parts
    core = lax.axis_index("tp")

    def within(value, slot):
        return lax.ppermute(value, "ctx", [(s, s ^ slot) for s in range(count)])

    def across(value, slot, step):
        perm = []
        for s in range(count):
            target = (s // parts + step) * parts + (s % parts ^ slot)
            if 0 <= target < count:
                perm.append((s, target))
        return lax.ppermute(value, "ctx", perm)

    def swapped(value):
        return lax.ppermute(value, "tp", [(0, 1), (1, 0)])

    wide = GROUP * rows
    span = parts * rows

    def pack(slots, crosses):
        shapes = [(2 * wide + 2 * rows, HD)] * len(slots) + [(2 * rows, HD)] * crosses
        return call(
            functools.partial(pack_kernel, parts, slots, crosses),
            [shape(dims) for dims in shapes],
            [ANY] * 4,
            [ANY] * len(shapes),
            scratch=[pltpu.VMEM(dims, jnp.bfloat16) for dims in shapes]
            + [pltpu.SemaphoreType.DMA((len(shapes), 2 * GROUP + 2)), pltpu.SemaphoreType.DMA((len(shapes),))],
            moved=2 << 20,
            room=56,
        )(attn_queries, attn_keys, attn_values, out_grad)

    full_2, full_3, full_1, full_0, *cross = pack((2, 3, 1, 0), parts)
    full = (full_0, full_1, full_2, full_3)
    got_cross = [across(cross[slot], slot, 1) for slot in range(parts)]
    got_full = [full[0]] + [within(full[slot], slot) for slot in range(1, parts)]

    half = rows // 2
    x_half = lax.dynamic_slice_in_dim(normed_input, core * half, half, 0)
    quarter = half // 2
    near_2 = within(x_half, 2)
    near_3 = within(x_half[:quarter], 3)
    near_1 = within(x_half, 1)
    relay = within(near_2[quarter:], 1)
    spots = ((2, 0), (3, 0), (1, 0), (3, quarter))
    x_pieces = []
    for piece in (near_2, near_3, near_1, relay):
        x_pieces += [piece, swapped(piece)]

    pairs = 2 * span * (parts + 1) * rows
    results = call(
        functools.partial(attention_kernel, parts, rows),
        [shape((parts * wide, HD)), shape((span, HD)), shape((span, HD))]
        + [shape((span, HD), jnp.float32)] * 2,
        [ANY] * (2 * parts),
        [VMEM] * 5,
        scratch=[
            pltpu.VMEM((parts * wide, HD), jnp.bfloat16),
            pltpu.VMEM((parts * wide, HD), jnp.bfloat16),
            pltpu.VMEM((2 * span, HD), jnp.bfloat16),
            pltpu.VMEM((2 * span, HD), jnp.bfloat16),
            pltpu.VMEM((2 * span, HD), jnp.float32),
            pltpu.VMEM((2 * span, HD), jnp.float32),
            pltpu.VMEM((2, span + rows, rows), jnp.float32),
            pltpu.VMEM((2, span + rows, rows), jnp.float32),
            pltpu.SemaphoreType.DMA((6 * parts,)),
        ],
        flops=10 * pairs * HD,
        moved=4 << 20,
        room=32,
    )(*got_full, *got_cross)
    dq, back_k, back_v, own_k, own_v = results
    got_k = across(back_k, 0, -1)
    got_v = across(back_v, 0, -1)

    def exchanged(values):
        return [values[0]] + [within(values[slot], slot) for slot in range(1, parts)]

    dq_parts = call(
        functools.partial(split_kernel, parts, wide), [shape((wide, HD))] * parts, [VMEM], [VMEM] * parts, moved=1 << 20
    )(dq)
    got_dq = exchanged(dq_parts)
    piece = features // count
    direct = blocks == 2
    terms = call(
        functools.partial(weight_kernel, parts, count, rows, spots),
        [shape((piece, HD))] * count if direct else [shape((features, HD))],
        [VMEM] * 2 + [ANY] * (1 + len(x_pieces)),
        [VMEM] * (count if direct else 1),
        scratch=[
            pltpu.VMEM((HD, span), jnp.bfloat16),
            pltpu.VMEM((span, features), jnp.bfloat16),
            pltpu.VMEM((features, HD), jnp.bfloat16),
            pltpu.SemaphoreType.DMA((1 + len(x_pieces),)),
        ],
        flops=2 * span * HD * features,
        moved=8 << 20,
        room=24,
    )(own_k, got_k, normed_input, *x_pieces)
    near_terms = terms[:parts] if direct else []
    got_terms = [within(terms[slot], slot) for slot in range(parts, count)] if direct else []
    dv_parts = call(
        functools.partial(value_kernel, parts, rows),
        [shape((rows + (piece if direct else 0), HD))] * parts,
        [VMEM] * (2 + len(near_terms)),
        [VMEM] * parts,
        moved=1 << 20,
    )(own_v, got_v, *near_terms)
    got_dv = exchanged(dv_parts)

    outs = call(
        functools.partial(spread_kernel, parts),
        [shape((rows, parts * GROUP * HD)), shape((rows, parts * HD))]
        + ([shape((piece, parts * HD), jnp.float32)] if direct else []),
        [VMEM] * (2 * parts + len(got_terms)),
        [VMEM] * (3 if direct else 2),
        moved=3 << 20,
    )(*got_dq, *got_dv, *got_terms)
    query_grad, value_grad = outs[:2]
    if direct:
        weight_grad = outs[2]
    else:
        pieces = terms[0].reshape(count, piece, HD)
        pieces = lax.all_to_all(pieces, "ctx", split_axis=0, concat_axis=0, tiled=True)
        pieces = pieces.reshape(blocks, parts, piece, HD).astype(jnp.float32)
        weight_grad = pieces.sum(axis=0).transpose(1, 0, 2).reshape(piece, parts * HD)
    return (query_grad, weight_grad, value_grad)


def solution(mesh):
    wide = P(("groups", "ctx"), "tp")

    return jax.shard_map(
        shards,
        mesh=mesh,
        in_specs=(P(("groups", "ctx"), None), wide, wide, wide, wide),
        out_specs=(wide, wide, wide),
        check_vma=False,
    )
```

```python
import functools

import jax
import jax.numpy as jnp
from jax import lax
from jax.experimental import pallas as pl
from jax.experimental.pallas import tpu as pltpu
from jax.sharding import PartitionSpec as P


HD = 128
HQ = 16
HK = 8
W = 1024
GROUP = HQ // HK

attn_scale = 168.0 ** (-0.5)
log2_e = 1.4426950408889634

VMEM = pl.BlockSpec(memory_space=pltpu.VMEM)
ANY = pl.BlockSpec(memory_space=pl.ANY)


def call(kernel, outs, in_specs, out_specs, scratch=(), flops=0, moved=0, room=8):
    return pl.pallas_call(
        kernel,
        out_shape=outs,
        in_specs=in_specs,
        out_specs=out_specs,
        scratch_shapes=list(scratch),
        cost_estimate=pl.CostEstimate(flops=flops, bytes_accessed=moved, transcendentals=0),
        compiler_params=pltpu.CompilerParams(vmem_limit_bytes=room << 20),
    )


def shape(dims, kind=jnp.bfloat16):
    return jax.ShapeDtypeStruct(dims, kind)


def place_of(parts):
    return lax.axis_index("ctx") % parts


def pack_kernel(parts, slots, crosses, q_ref, k_ref, v_ref, d_ref, *refs):
    count = len(slots) + crosses
    outs, held, sems, out_sems = refs[:count], refs[count : 2 * count], refs[-2], refs[-1]
    rows = q_ref.shape[0]
    copies = []
    for at in range(count):
        cross = at >= len(slots)
        head = place_of(parts) ^ (at - len(slots) if cross else slots[at])
        sources = [(k_ref, head), (v_ref, head)]
        if not cross:
            sources = [(ref, head * GROUP + g) for ref in (q_ref, d_ref) for g in range(GROUP)] + sources
        mine = []
        for step, (ref, column) in enumerate(sources):
            source = ref.at[:, pl.ds(pl.multiple_of(column * HD, HD), HD)]
            target = held[at].at[step * rows : (step + 1) * rows]
            copy = pltpu.make_async_copy(source, target, sems.at[at, step])
            copy.start()
            mine.append(copy)
        copies.append(mine)
    sent = []
    for at, mine in enumerate(copies):
        for copy in mine:
            copy.wait()
        copy = pltpu.make_async_copy(held[at], outs[at], out_sems.at[at])
        copy.start()
        sent.append(copy)
    for copy in sent:
        copy.wait()


def attention_kernel(parts, rows, *refs):
    full, cross = refs[:parts], refs[parts : 2 * parts]
    dq_s, back_k, back_v, own_k, own_v = refs[2 * parts : 2 * parts + 5]
    q_s, d_s, k_s, v_s, dk_s, dv_s, s_s, p_s, sems = refs[2 * parts + 5 :]
    place = place_of(parts)
    first = lax.axis_index("ctx") < parts
    span = parts * rows
    wide = GROUP * rows
    copies = []

    def move(source, target):
        copy = pltpu.make_async_copy(source, target, sems.at[len(copies)])
        copy.start()
        copies.append(copy)

    for slot in range(parts):
        spot = place ^ slot
        pair = pl.ds(pl.multiple_of(spot * wide, wide), wide)
        old = pl.ds(pl.multiple_of(spot * rows, rows), rows)
        new = pl.ds(pl.multiple_of(span + spot * rows, rows), rows)
        move(full[slot].at[0:wide], q_s.at[pair])
        move(full[slot].at[wide : 2 * wide], d_s.at[pair])
        move(full[slot].at[2 * wide : 2 * wide + rows], k_s.at[new])
        move(full[slot].at[2 * wide + rows : 2 * wide + 2 * rows], v_s.at[new])
        move(cross[slot].at[0:rows], k_s.at[old])
        move(cross[slot].at[rows : 2 * rows], v_s.at[old])
    dk_s[...] = jnp.zeros_like(dk_s)
    dv_s[...] = jnp.zeros_like(dv_s)
    for copy in copies:
        copy.wait()

    key_at = lax.broadcasted_iota(jnp.int32, (rows, rows), 0)
    older = key_at > lax.broadcasted_iota(jnp.int32, (rows, rows), 1)
    nt = (((1,), (1,)), ((), ()))
    chunks = parts + 1
    hidden = jnp.float32(-jnp.inf)

    def queries_of(task):
        at = (task // GROUP) * wide + (task % GROUP) * rows
        return slice(at, at + rows)

    def keys_of(task, chunk):
        at = (task // GROUP + chunk) * rows
        return slice(at, at + rows)

    def held(chunk):
        return slice(chunk * rows, (chunk + 1) * rows)

    def scores(task, chunk):
        keys, slot = keys_of(task, chunk), task % 2
        s = lax.dot_general(k_s[keys, :], q_s[queries_of(task), :], nt, preferred_element_type=jnp.float32)
        s = s * (attn_scale * log2_e)
        if chunk == 0:
            s = jnp.where(older, s, hidden)
        if chunk == chunks - 1:
            s = jnp.where(older, hidden, s)
        s_s[slot, held(chunk), :] = s
        p_s[slot, held(chunk), :] = lax.dot_general(
            v_s[keys, :], d_s[queries_of(task), :], nt, preferred_element_type=jnp.float32
        )
        return jnp.max(s, axis=0, keepdims=True)

    def all_tasks(skipped):
        count = parts * GROUP

        def used(task):
            return [chunk for chunk in range(chunks) if task // GROUP + chunk >= skipped]

        top = functools.reduce(jnp.maximum, [scores(0, chunk) for chunk in used(0)])
        for task in range(count):
            slot = task % 2
            total = jnp.zeros((1, rows), jnp.float32)
            delta = jnp.zeros((1, rows), jnp.float32)
            tops = []
            following = list(used(task + 1)) if task + 1 < count else []
            for chunk in used(task):
                e = jnp.exp2(s_s[slot, held(chunk), :] - top)
                s_s[slot, held(chunk), :] = e
                total = total + jnp.sum(e, axis=0, keepdims=True)
                delta = delta + jnp.sum(e * p_s[slot, held(chunk), :], axis=0, keepdims=True)
                if following:
                    tops.append(scores(task + 1, following.pop(0)))
            inverse = 1.0 / total
            delta = delta * inverse
            dq = jnp.zeros((HD, rows), jnp.float32)
            for chunk in used(task):
                soft = s_s[slot, held(chunk), :] * inverse
                ds = (soft * (p_s[slot, held(chunk), :] - delta)).astype(jnp.bfloat16)
                low = soft.astype(jnp.bfloat16)
                here = keys_of(task, chunk)
                dv_s[here, :] += jnp.dot(low, d_s[queries_of(task), :], preferred_element_type=jnp.float32)
                dk_s[here, :] += jnp.dot(ds, q_s[queries_of(task), :], preferred_element_type=jnp.float32)
                dq += lax.dot_general(
                    k_s[here, :], ds, (((0,), (0,)), ((), ())), preferred_element_type=jnp.float32
                )
                if following:
                    tops.append(scores(task + 1, following.pop(0)))
            dq_s[queries_of(task), :] = (attn_scale * dq).T.astype(jnp.bfloat16)
            while following:
                tops.append(scores(task + 1, following.pop(0)))
            if tops:
                top = functools.reduce(jnp.maximum, tops)

    for skipped, here in ((parts, first), (0, jnp.logical_not(first))):

        @pl.when(here)
        def _(skipped=skipped):
            all_tasks(skipped)

    back_k[...] = (attn_scale * dk_s[:span, :]).astype(jnp.bfloat16)
    own_k[...] = attn_scale * dk_s[span:, :]
    back_v[...] = dv_s[:span, :].astype(jnp.bfloat16)
    own_v[...] = dv_s[span:, :]


def weight_kernel(parts, count, rows, spots, own_k, back_k, x_own, *refs):
    pieces, outs = refs[: 2 * len(spots)], refs[2 * len(spots) : -4]
    dk_s, x_s, w_s, sems = refs[-4:]
    place, core = place_of(parts), lax.axis_index("tp")
    half = rows // 2
    copies = []

    def move(source, at):
        target = x_s.at[pl.ds(pl.multiple_of(at, 64), source.shape[0])]
        copy = pltpu.make_async_copy(source, target, sems.at[len(copies)])
        copy.start()
        copies.append(copy)

    move(x_own, place * rows)
    for at, (slot, offset) in enumerate(spots):
        base = (place ^ slot) * rows + offset
        move(pieces[2 * at], base + core * half)
        move(pieces[2 * at + 1], base + (1 - core) * half)
    dk_s[...] = (own_k[...] + back_k[...].astype(jnp.float32)).astype(jnp.bfloat16).T
    for copy in copies:
        copy.wait()
    total = jnp.dot(dk_s[...], x_s[...], preferred_element_type=jnp.float32)
    if len(outs) == 1:
        outs[0][...] = total.T.astype(jnp.bfloat16)
        return
    w_s[...] = total.T.astype(jnp.bfloat16)
    piece = w_s.shape[0] // count
    for slot in range(count):
        at = (lax.axis_index("ctx") ^ slot) * piece
        outs[slot][...] = w_s[pl.ds(pl.multiple_of(at, 16), piece), :]


def split_kernel(parts, rows, value, *outs):
    for slot in range(parts):
        at = (place_of(parts) ^ slot) * rows
        outs[slot][...] = value[pl.ds(pl.multiple_of(at, rows), rows), :]


def value_kernel(parts, rows, own_v, back_v, *refs):
    terms, outs = refs[:-parts], refs[-parts:]
    for slot in range(parts):
        at = pl.ds(pl.multiple_of((place_of(parts) ^ slot) * rows, rows), rows)
        outs[slot][:rows, :] = (own_v[at, :] + back_v[at, :].astype(jnp.float32)).astype(jnp.bfloat16)
        if terms:
            outs[slot][rows:, :] = terms[slot][...]


def query_kernel(parts, *refs):
    out = refs[-1]
    rows = out.shape[0]
    for slot in range(parts):
        head = place_of(parts) ^ slot
        for g in range(GROUP):
            at = pl.ds(pl.multiple_of((head * GROUP + g) * HD, HD), HD)
            out[:, at] = refs[slot][g * rows : (g + 1) * rows, :]


def spread_kernel(parts, rows, *refs):
    dv = refs[:parts]
    outs = refs[-2:] if len(refs) > parts + 1 else refs[-1:]
    terms = refs[parts : -len(outs)]
    for slot in range(parts):
        head = place_of(parts) ^ slot
        at = pl.ds(pl.multiple_of(head * HD, HD), HD)
        outs[0][:, at] = dv[slot][:rows, :]
        if terms:
            outs[1][:, at] = dv[slot][rows:, :].astype(jnp.float32) + terms[slot][...].astype(jnp.float32)


def shards(normed_input, attn_queries, attn_keys, attn_values, out_grad):
    rows, features = normed_input.shape
    heads = attn_keys.shape[1] // HD
    count = lax.axis_size("ctx")
    parts = W // rows
    assert parts == heads and count % parts == 0 and parts & (parts - 1) == 0
    blocks = count // parts
    core = lax.axis_index("tp")

    def within(value, slot):
        return lax.ppermute(value, "ctx", [(s, s ^ slot) for s in range(count)])

    def across(value, slot, step):
        perm = []
        for s in range(count):
            target = (s // parts + step) * parts + (s % parts ^ slot)
            if 0 <= target < count:
                perm.append((s, target))
        return lax.ppermute(value, "ctx", perm)

    def swapped(value):
        return lax.ppermute(value, "tp", [(0, 1), (1, 0)])

    wide = GROUP * rows
    span = parts * rows

    def pack(slots, crosses):
        shapes = [(2 * wide + 2 * rows, HD)] * len(slots) + [(2 * rows, HD)] * crosses
        return call(
            functools.partial(pack_kernel, parts, slots, crosses),
            [shape(dims) for dims in shapes],
            [ANY] * 4,
            [ANY] * len(shapes),
            scratch=[pltpu.VMEM(dims, jnp.bfloat16) for dims in shapes]
            + [pltpu.SemaphoreType.DMA((len(shapes), 2 * GROUP + 2)), pltpu.SemaphoreType.DMA((len(shapes),))],
            moved=2 << 20,
            room=56,
        )(attn_queries, attn_keys, attn_values, out_grad)

    full_2, full_3, full_1, full_0, *cross = pack((2, 3, 1, 0), parts)
    full = (full_0, full_1, full_2, full_3)
    got_cross = [across(cross[slot], slot, 1) for slot in range(parts)]
    got_full = [full[0]] + [within(full[slot], slot) for slot in range(1, parts)]

    half = rows // 2
    x_half = lax.dynamic_slice_in_dim(normed_input, core * half, half, 0)
    quarter = half // 2
    near_2 = within(x_half, 2)
    near_3 = within(x_half[:quarter], 3)
    near_1 = within(x_half, 1)
    relay = within(near_2[quarter:], 1)
    spots = ((2, 0), (3, 0), (1, 0), (3, quarter))
    x_pieces = []
    for piece in (near_2, near_3, near_1, relay):
        x_pieces += [piece, swapped(piece)]

    pairs = 2 * span * (parts + 1) * rows
    results = call(
        functools.partial(attention_kernel, parts, rows),
        [shape((parts * wide, HD)), shape((span, HD)), shape((span, HD))]
        + [shape((span, HD), jnp.float32)] * 2,
        [ANY] * (2 * parts),
        [VMEM] * 5,
        scratch=[
            pltpu.VMEM((parts * wide, HD), jnp.bfloat16),
            pltpu.VMEM((parts * wide, HD), jnp.bfloat16),
            pltpu.VMEM((2 * span, HD), jnp.bfloat16),
            pltpu.VMEM((2 * span, HD), jnp.bfloat16),
            pltpu.VMEM((2 * span, HD), jnp.float32),
            pltpu.VMEM((2 * span, HD), jnp.float32),
            pltpu.VMEM((2, span + rows, rows), jnp.float32),
            pltpu.VMEM((2, span + rows, rows), jnp.float32),
            pltpu.SemaphoreType.DMA((6 * parts,)),
        ],
        flops=10 * pairs * HD,
        moved=4 << 20,
        room=32,
    )(*got_full, *got_cross)
    dq, back_k, back_v, own_k, own_v = results
    got_k = across(back_k, 0, -1)
    got_v = across(back_v, 0, -1)

    def exchanged(values):
        return [values[0]] + [within(values[slot], slot) for slot in range(1, parts)]

    dq_parts = call(
        functools.partial(split_kernel, parts, wide), [shape((wide, HD))] * parts, [VMEM], [VMEM] * parts, moved=1 << 20
    )(dq)
    got_dq = exchanged(dq_parts)
    piece = features // count
    direct = blocks == 2
    terms = call(
        functools.partial(weight_kernel, parts, count, rows, spots),
        [shape((piece, HD))] * count if direct else [shape((features, HD))],
        [VMEM] * 2 + [ANY] * (1 + len(x_pieces)),
        [VMEM] * (count if direct else 1),
        scratch=[
            pltpu.VMEM((HD, span), jnp.bfloat16),
            pltpu.VMEM((span, features), jnp.bfloat16),
            pltpu.VMEM((features, HD), jnp.bfloat16),
            pltpu.SemaphoreType.DMA((1 + len(x_pieces),)),
        ],
        flops=2 * span * HD * features,
        moved=8 << 20,
        room=24,
    )(own_k, got_k, normed_input, *x_pieces)
    near_terms = terms[:parts] if direct else []
    got_terms = [within(terms[slot], slot) for slot in range(parts, count)] if direct else []
    dv_parts = call(
        functools.partial(value_kernel, parts, rows),
        [shape((rows + (piece if direct else 0), HD))] * parts,
        [VMEM] * (2 + len(near_terms)),
        [VMEM] * parts,
        moved=1 << 20,
    )(own_v, got_v, *near_terms)
    got_dv = exchanged(dv_parts)

    query_grad = call(
        functools.partial(query_kernel, parts), shape((rows, parts * GROUP * HD)), [VMEM] * parts, VMEM, moved=1 << 20
    )(*got_dq)
    outs = call(
        functools.partial(spread_kernel, parts, rows),
        [shape((rows, parts * HD))] + ([shape((piece, parts * HD), jnp.float32)] if direct else []),
        [VMEM] * (parts + len(got_terms)),
        [VMEM] * (2 if direct else 1),
        moved=2 << 20,
    )(*got_dv, *got_terms)
    value_grad = outs[0]
    if direct:
        weight_grad = outs[1]
    else:
        pieces = terms[0].reshape(count, piece, HD)
        pieces = lax.all_to_all(pieces, "ctx", split_axis=0, concat_axis=0, tiled=True)
        pieces = pieces.reshape(blocks, parts, piece, HD).astype(jnp.float32)
        weight_grad = pieces.sum(axis=0).transpose(1, 0, 2).reshape(piece, parts * HD)
    return (query_grad, weight_grad, value_grad)


def solution(mesh):
    wide = P(("groups", "ctx"), "tp")

    return jax.shard_map(
        shards,
        mesh=mesh,
        in_specs=(P(("groups", "ctx"), None), wide, wide, wide, wide),
        out_specs=(wide, wide, wide),
        check_vma=False,
    )
```
